32 devices in a mesh: wide: 16 (over z, x, core), narrow: 2 (over y).
Axes of the slice: x: 2, y: 2, z: 4, core: 2. Of those that a mesh axis runs over, the one named last changes fastest.
Arguments:
- embeddings: float32 [16384, 512], P(('wide', 'narrow')), may hold values from -2.1 to 2.1
- accum: float32 [16384], P(('wide', 'narrow')), may hold values from 0.01 to 1
- relation: bfloat16 [512, 512], replicated, may hold values from -0.25 to 0.25
- head_index: int32 [2, 16384], P(None, ('wide', 'narrow')), may hold values from 0 to 511
- tail_index: int32 [2, 16384], P(None, ('wide', 'narrow')), may hold values from 0 to 511
- negative_index: int32 [2, 8192], P(None, ('wide', 'narrow')), may hold values from 0 to 511
- partner: int32 [2, 16], replicated, may hold values from 0 to 15, each once within a row
- edge_count: int32 [2, 32], P(None, ('wide', 'narrow')), may hold values from 1 to 512, 8192 in all within a row
Outputs:
- new_embeddings: float32 [16384, 512], P(('wide', 'narrow'))
- new_accum: float32 [16384], P(('wide', 'narrow'))
- relation_grad: float32 [512, 512], replicated
- edge_losses: float32 [2, 16384], P(None, ('wide', 'narrow'))
The draws below stay inside these ranges and needn't reach their ends.
Inputs may be any that keep to these rules, and one draw needn't show every extreme that they name: Each row of partner is a permutation of the wide indices. `edge_count`: in each bucket step the counts of all devices sum to half of all slots, and some device has exactly 512.
All inputs are finite; a program needn't handle non-finite values.
Results may differ from the reference program's by a relative error of at most 0.0064.
Values may be sent and summed in bfloat16 or wider, within the bound.
A program may use at most 64 MiB of HBM per device.

```python
import math
import jax
import jax.numpy as jnp
import numpy as np
from jax import lax

D = 512
BLOCK = 512
EDGES = 512
NEG_DEV = 256
STEPS = 2
ENTITIES = 16384
N_WIDE = 16
N_NARROW = 2


def plant(result, stream_key, least, largest):
    dims = result.shape
    place = [jax.random.randint(jax.random.fold_in(stream_key, axis), (), 0, dims[axis]) for axis in range(len(dims))]
    result = result.at[tuple(place)].set(least)
    longest = dims.index(max(dims))
    place[longest] = (place[longest] + 1) % dims[longest]
    return result.at[tuple(place)].set(largest)


def block_levels(own_key, extent, cuts, smallest, top_value):
    gain, own = 1.0, jax.random.fold_in(own_key, 6)
    for axis_at, blocks in cuts:
        draws = jnp.exp(jax.random.uniform(jax.random.fold_in(own, axis_at), (blocks,), jnp.float32, smallest / len(cuts), top_value / len(cuts)))
        gain = gain * jnp.repeat(draws, extent[axis_at] // blocks).reshape([-1 if axis == axis_at else 1 for axis in range(len(extent))])
    return gain


def rank_bounds(amount, slope):
    loads = [(1 << 20) // math.isqrt(grade ** slope) + 1 for grade in range(1, amount + 1)]
    spread = 1 + sum(loads) // (1 << 30)
    return np.cumsum(np.array([max(1, weight // spread) for weight in loads]))


def ranked_ids(own_key, extent, number_of, skew):
    table = rank_bounds(number_of, skew)
    lot = jax.random.randint(jax.random.fold_in(own_key, 1), extent, 0, int(table[number_of - 1]))
    rank = jnp.searchsorted(jnp.asarray(table, jnp.int32), lot, side="right")
    return jax.random.permutation(jax.random.fold_in(own_key, 2), number_of)[rank].astype(jnp.int32)


def length_profile(amount, total, reach, lean):
    weights = [(1 << 20) // math.isqrt(standing ** lean) + 1 for standing in range(2, amount + 1)]
    rest, holding = total - reach - (amount - 1), [1] * (amount - 1)
    while rest > 0:
        movable = [i for i in range(amount - 1) if holding[i] < reach]
        mass, left = sum([weights[i] for i in movable]), rest
        for i in movable:
            addition = min(reach - holding[i], max(1, left * weights[i] // mass), rest)
            holding[i] = holding[i] + addition
            rest = rest - addition
    return np.array([reach] + holding)


def ragged_sizes(own_key, count, total, limit, lean):
    if count == 2:
        one = jax.random.randint(own_key, (), max(1, total - limit), min(limit, total - 1) + 1)
        return jnp.stack([one, total - one])
    tallies = jnp.asarray(length_profile(count, total, limit, lean), jnp.int32)
    twos = (count - 1) // 2
    source_of, receiver = tallies[1:1 + 2 * twos:2], tallies[2:2 + 2 * twos:2]
    slack = jnp.minimum(source_of - 1, limit - receiver)
    moved = jax.random.randint(jax.random.fold_in(own_key, 1), (twos,), 0, 1 << 20) % (slack + 1)
    tallies = tallies.at[1:1 + 2 * twos:2].set(source_of - moved).at[2:2 + 2 * twos:2].set(receiver + moved)
    return tallies[jax.random.permutation(jax.random.fold_in(own_key, 2), count)]


def noise(key, dims, spread, most, pieces=(), kind=jnp.bfloat16):
    drawn = jax.random.normal(key, dims, jnp.float32) * spread
    if len(pieces) > 0:
        drawn = block_levels(key, dims, pieces, -0.22, 0.18) * drawn
    return jnp.clip(drawn, min=-most, max=most).astype(kind)


def setup_inputs(seed: int = 0) -> dict:
    keys = jax.random.split(jax.random.key(seed), 9)
    embeddings = noise(keys[0], (ENTITIES, D), 0.35, 2.1, ((0, 32),), jnp.float32)
    accum = jnp.clip(jnp.exp(math.log(1.0) - 4.6051702 * jax.random.uniform(keys[1], (ENTITIES,), jnp.float32) ** block_levels(keys[1], (ENTITIES,), ((0, 32),), -0.2, 0.2)), 0.01, 1.0)
    relation = noise(keys[2], (D, D), D ** -0.5, 0.25)
    head_index = plant(jax.random.randint(keys[3], (STEPS, EDGES * N_WIDE * N_NARROW), 0, BLOCK), jax.random.fold_in(keys[3], 1), 0, BLOCK - 1).astype(jnp.int32)
    tail_index = plant(ranked_ids(keys[4], (STEPS, EDGES * N_WIDE * N_NARROW), BLOCK, 1), jax.random.fold_in(keys[4], 3), 0, BLOCK - 1).astype(jnp.int32)
    negative_index = plant(jax.random.randint(keys[5], (STEPS, NEG_DEV * N_WIDE * N_NARROW), 0, BLOCK), jax.random.fold_in(keys[5], 1), 0, BLOCK - 1).astype(jnp.int32)
    partner = jax.vmap(lambda own: jax.random.permutation(own, N_WIDE))(jax.random.split(keys[6], STEPS)).reshape((STEPS, N_WIDE)).astype(jnp.int32)
    edge_count = jax.vmap(lambda own: ragged_sizes(own, N_WIDE * N_NARROW, EDGES * N_WIDE * N_NARROW // 2, EDGES, 2))(jax.random.split(keys[7], STEPS)).reshape((STEPS, N_WIDE * N_NARROW)).astype(jnp.int32)
    return dict(embeddings=embeddings, accum=accum, relation=relation, head_index=head_index, tail_index=tail_index, negative_index=negative_index, partner=partner, edge_count=edge_count)


LEARN_RATE = 0.1
EPSILON = 1e-06

def widen(values):
    return lax.optimization_barrier(values).astype(jnp.float32)

def take_rows(block, indices):
    return jnp.take(block, indices.astype(jnp.int32), axis=0)

def scatter_one(indices, rows):
    return jnp.zeros((BLOCK, rows.shape[-1]), rows.dtype).at[indices].add(rows)

def scatter_two(first_ids, first_rows, second_ids, second_rows):
    return scatter_one(first_ids, first_rows).at[second_ids].add(second_rows)

def reference(embeddings, accum, relation, head_index, tail_index, negative_index, partner, edge_count):
    wide, narrow = (N_WIDE, N_NARROW)
    table = embeddings.reshape(wide, narrow, BLOCK, D)
    rates = accum.reshape(wide, narrow, BLOCK)
    relation_f = relation.astype(jnp.float32)
    relation_sum = jnp.zeros((D, D), jnp.float32)
    loss_rows = []
    for step in range(STEPS):
        heads = head_index[step].reshape(wide, narrow, EDGES)
        tails = tail_index[step].reshape(wide, narrow, EDGES)
        negs = negative_index[step].reshape(wide, narrow, NEG_DEV)
        counts = edge_count[step].reshape(wide, narrow)
        table_bf = table.astype(jnp.bfloat16)
        order = partner[step]

        def group(index):
            own = table_bf[index]
            served = table_bf[order[index]]
            head_rows = widen(jax.vmap(take_rows)(own, heads[index]))
            live = jnp.arange(EDGES, dtype=jnp.int32)[None, :] < counts[index][:, None]
            query = jnp.einsum('nek,kj->nej', head_rows, relation_f)
            query_f = widen(jnp.where(live[..., None], query, 0.0).astype(jnp.bfloat16))
            tail_rows = widen(jax.vmap(take_rows)(served, tails[index]))
            negatives = widen(jax.vmap(take_rows)(served, negs[index])).reshape(narrow * NEG_DEV, D)
            positive = lax.optimization_barrier(jnp.sum(query_f * tail_rows, axis=-1))
            scores = jnp.einsum('nek,mk->nem', query_f, negatives)
            exp_pos = jnp.exp(positive)
            exp_neg = jnp.exp(scores)
            total = exp_pos + lax.optimization_barrier(jnp.sum(exp_neg, axis=-1))
            losses = jnp.log(total) - positive
            pos_weight = exp_pos / total - 1.0
            weights = widen((exp_neg / total[..., None]).astype(jnp.bfloat16))
            query_grad = pos_weight[..., None] * tail_rows + jnp.einsum('nem,mk->nek', weights, negatives)
            tail_pos = pos_weight[..., None] * query_f
            partial_terms = widen(jnp.einsum('nem,nek->nmk', weights, query_f).astype(jnp.bfloat16))
            negative_grad = lax.optimization_barrier(jnp.sum(partial_terms, axis=0)).reshape(narrow, NEG_DEV, D)
            tail_grad = jax.vmap(scatter_two)(tails[index], tail_pos, negs[index], negative_grad)
            grad_f = widen(jnp.where(live[..., None], query_grad, 0.0).astype(jnp.bfloat16))
            head_term = jnp.einsum('nek,jk->nej', grad_f, relation_f)
            head_grad = jax.vmap(scatter_one)(heads[index], head_term)
            relation_part = jnp.einsum('nej,nek->jk', head_rows, grad_f)
            return (head_grad, tail_grad, relation_part, jnp.where(live, losses, 0.0))
        head_grads, tail_grads, parts, losses = lax.map(group, jnp.arange(wide, dtype=jnp.int32))
        owner_grads = jnp.zeros_like(tail_grads).at[order].set(tail_grads)
        relation_sum = relation_sum + lax.optimization_barrier(jnp.sum(parts, axis=0))
        grads = head_grads + owner_grads
        rates = rates + lax.optimization_barrier(jnp.mean(grads * grads, axis=-1))
        table = table - LEARN_RATE * grads / (jnp.sqrt(rates)[..., None] + EPSILON)
        loss_rows.append(losses.reshape(-1))
    return (table.reshape(wide * narrow * BLOCK, D), rates.reshape(-1), relation_sum, jnp.stack(loss_rows))
```

```python
import functools

import jax
import jax.numpy as jnp
from jax import lax
from jax.experimental import pallas as pl
from jax.experimental.pallas import tpu as pltpu
from jax.sharding import PartitionSpec as P

LEARN_RATE = 0.1
EPSILON = 1e-06
MESH = pl.DeviceIdType.MESH
F32 = jnp.float32
BF16 = jnp.bfloat16

QUERY_OUT, QUERY_IN, GRAD_OUT, GRAD_IN, LOSS = range(5)
NEG, NEG_GRAD = range(2)
TAIL_IDS, NEG_IDS, REL_SUM, REL_GROUP, REL_ALL = range(5)


def dot(a, b, contract):
    return lax.dot_general(a, b, (contract, ((), ())), preferred_element_type=F32)


def one_hot_t(row, rows):
    number = lax.broadcasted_iota(jnp.int32, (rows, row.shape[1]), 0)
    return jnp.where(number == row, 1.0, 0.0).astype(BF16)


def to_row(column):
    return jnp.transpose(jnp.broadcast_to(column, (column.shape[0], 128)))[:1, :]


def to_column(row):
    return jnp.transpose(jnp.broadcast_to(row, (128, row.shape[1])))[:, :1]


def kernel(
    wide, narrow, chunk,
    emb_ref, acc_ref, rel_ref, head_ref, tail_ref, neg_ref, partner_ref, inverse_ref, count_ref,
    emb_out, acc_out, rel_out, loss_out,
    tail_all, neg_all, table, head_t, tail_t, neg_t, head_rows, tail_rows,
    q_send, q_mid, q_mid_send, q_recv, g_send, g_mid, g_mid_send, g_recv,
    loss_send, loss_all, negs, ng_send, ng_recv, weights, tail_pos, tail_grad,
    rel_acc, rel_send, rel_recv, rel_group_send, rel_group, rel_all_send, rel_all,
    send_sem, recv_sem, nsend_sem, nrecv_sem, xsend_sem, xrecv_sem,
):
    w = lax.axis_index("wide")
    n = lax.axis_index("narrow")
    steps, edges = head_ref.shape
    block, width = emb_ref.shape
    negatives = neg_ref.shape[1]

    barrier = pltpu.get_barrier_semaphore()

    def greet_wide(i, carry):
        pl.semaphore_signal(
            barrier, inc=1, device_id=(lax.rem(w + i, wide), n), device_id_type=MESH
        )
        return carry

    def greet_narrow(i, carry):
        pl.semaphore_signal(
            barrier, inc=1, device_id=(w, lax.rem(n + i, narrow)), device_id_type=MESH
        )
        return carry

    lax.fori_loop(1, wide, greet_wide, 0)
    lax.fori_loop(1, narrow, greet_narrow, 0)
    pl.semaphore_wait(barrier, wide + narrow - 2)

    def wide_start(source, target, ssem, rsem):
        def go(i, carry):
            j = lax.rem(w + i, wide)
            pltpu.make_async_remote_copy(
                src_ref=source(j), dst_ref=target(w), send_sem=ssem, recv_sem=rsem,
                device_id=(j, n), device_id_type=MESH,
            ).start()
            return carry

        lax.fori_loop(1, wide, go, 0)

    def narrow_start(source, target, ssem, rsem):
        def go(i, carry):
            j = lax.rem(n + i, narrow)
            pltpu.make_async_remote_copy(
                src_ref=source(j), dst_ref=target(n), send_sem=ssem, recv_sem=rsem,
                device_id=(w, j), device_id_type=MESH,
            ).start()
            return carry

        lax.fori_loop(1, narrow, go, 0)

    def wait(slots, sem):
        pltpu.make_async_copy(slots, slots, sem).wait()

    wide_start(
        lambda j: tail_ref, lambda m: tail_all.at[m], xsend_sem.at[TAIL_IDS], xrecv_sem.at[TAIL_IDS]
    )
    wide_start(
        lambda j: neg_ref, lambda m: neg_all.at[m], xsend_sem.at[NEG_IDS], xrecv_sem.at[NEG_IDS]
    )
    tail_all[w] = tail_ref[...]
    neg_all[w] = neg_ref[...]
    emb_out[...] = emb_ref[...]
    acc_out[...] = acc_ref[...]
    rel_acc[...] = jnp.zeros_like(rel_acc)
    others = pl.ds(0, wide - 1)
    peers = pl.ds(0, narrow - 1)

    def step(s, carry):
        row = pl.ds(s, 1)
        count = count_ref[s, 0]
        table[...] = emb_out[...].astype(BF16)
        head_t[...] = one_hot_t(head_ref[row, :], block)
        head_rows[...] = dot(head_t[...], table[...], ((0,), (0,))).astype(BF16)
        query = dot(head_rows[...], rel_ref[...], ((1,), (0,)))
        live = lax.broadcasted_iota(jnp.int32, (edges, width), 0) < count
        q_send[s] = jnp.where(live, query, 0.0).astype(BF16).reshape(q_send.shape[1:])
        wide_start(
            lambda j: q_send.at[s, j], lambda m: q_mid.at[s, m],
            send_sem.at[s, QUERY_OUT], recv_sem.at[s, QUERY_OUT],
        )
        q_mid[s, w] = q_send[s, w]

        @pl.when(s == 0)
        def _():
            wait(tail_all.at[others], xrecv_sem.at[TAIL_IDS])
            wait(neg_all.at[others], xrecv_sem.at[NEG_IDS])

        user = inverse_ref[s, w]
        neg_t[...] = one_hot_t(neg_all[user, row, :], block)
        negs[s, n] = dot(neg_t[...], table[...], ((0,), (0,))).astype(BF16)
        narrow_start(
            lambda j: negs.at[s, n], lambda m: negs.at[s, m],
            nsend_sem.at[s, NEG], nrecv_sem.at[s, NEG],
        )
        tail_t[...] = one_hot_t(tail_all[user, row, :], block)
        tail_rows[...] = dot(tail_t[...], table[...], ((0,), (0,))).astype(BF16)

        wait(q_mid.at[s, others], recv_sem.at[s, QUERY_OUT])

        def relay_query(j, c):
            q_mid_send[s, j] = q_mid[s, inverse_ref[s, j]]
            return c

        lax.fori_loop(0, wide, relay_query, 0)
        wide_start(
            lambda j: q_mid_send.at[s, j], lambda m: q_recv.at[s, m],
            send_sem.at[s, QUERY_IN], recv_sem.at[s, QUERY_IN],
        )
        q_recv[s, w] = q_mid_send[s, w]
        wait(negs.at[s, peers], nrecv_sem.at[s, NEG])
        wait(q_recv.at[s, others], recv_sem.at[s, QUERY_IN])

        shared = negs[s].reshape(narrow * negatives, width)
        pieces = chunk // q_recv.shape[2]
        for c in range(edges // chunk):
            part = slice(c * chunk, (c + 1) * chunk)
            part3 = slice(c * pieces, (c + 1) * pieces)
            q = q_recv[s, part3].reshape(chunk, width)
            q32 = q.astype(F32)
            t32 = tail_rows[part, :].astype(F32)
            positive = jnp.sum(q32 * t32, axis=1, keepdims=True)
            exp_neg = jnp.exp(dot(q, shared, ((1,), (1,))))
            exp_pos = jnp.exp(positive)
            total = exp_pos + jnp.sum(exp_neg, axis=1, keepdims=True)
            pos_weight = exp_pos / total - 1.0
            wts = (exp_neg * (1.0 / total)).astype(BF16)
            weights[part, :] = wts
            grad = pos_weight * t32 + dot(wts, shared, ((1,), (0,)))
            g_send[s, part3] = grad.astype(BF16).reshape(pieces, q_recv.shape[2], width)
            tail_pos[part, :] = (pos_weight * q32).astype(BF16)
            loss_send[s, :, part] = to_row(jnp.log(total) - positive)
        wide_start(
            lambda j: g_send.at[s, j], lambda m: g_mid.at[s, m],
            send_sem.at[s, GRAD_OUT], recv_sem.at[s, GRAD_OUT],
        )
        g_mid[s, w] = g_send[s, w]
        queries = q_recv[s].reshape(edges, width)
        for k in range(narrow):
            cols = slice(k * negatives, (k + 1) * negatives)
            ng_send[s, k] = dot(weights[:, cols], queries, ((0,), (0,))).astype(BF16)
        narrow_start(
            lambda j: ng_send.at[s, j], lambda m: ng_recv.at[s, m],
            nsend_sem.at[s, NEG_GRAD], nrecv_sem.at[s, NEG_GRAD],
        )
        ng_recv[s, n] = ng_send[s, n]
        wide_start(
            lambda j: loss_send.at[s], lambda m: loss_all.at[s, m],
            send_sem.at[s, LOSS], recv_sem.at[s, LOSS],
        )
        loss_all[s, w] = loss_send[s]
        tail_grad[...] = dot(tail_t[...], tail_pos[...], ((1,), (0,)))

        wait(g_mid.at[s, others], recv_sem.at[s, GRAD_OUT])

        def relay_grad(j, c):
            g_mid_send[s, j] = g_mid[s, partner_ref[s, j]]
            return c

        lax.fori_loop(0, wide, relay_grad, 0)
        wide_start(
            lambda j: g_mid_send.at[s, j], lambda m: g_recv.at[s, m],
            send_sem.at[s, GRAD_IN], recv_sem.at[s, GRAD_IN],
        )
        g_recv[s, w] = g_mid_send[s, w]

        wait(ng_recv.at[s, peers], nrecv_sem.at[s, NEG_GRAD])
        for k in range(narrow):
            tail_grad[...] += dot(neg_t[...], ng_recv[s, k], ((1,), (0,)))
        wait(loss_all.at[s, others], recv_sem.at[s, LOSS])
        losses = loss_all[s, partner_ref[s, w]]
        live_row = lax.broadcasted_iota(jnp.int32, (1, edges), 1) < count
        loss_out[row, :] = jnp.where(live_row, losses, 0.0)

        wait(g_recv.at[s, others], recv_sem.at[s, GRAD_IN])
        back = g_recv[s].reshape(edges, width)
        grad_bf = jnp.where(live, back.astype(F32), 0.0).astype(BF16)
        rel_acc[...] += dot(head_rows[...], grad_bf, ((0,), (0,)))

        @pl.when(s == steps - 1)
        def _():
            rel_send[...] = rel_acc[...].astype(BF16).reshape(rel_send.shape)
            wide_start(
                lambda j: rel_send.at[j], lambda m: rel_recv.at[m],
                xsend_sem.at[REL_SUM], xrecv_sem.at[REL_SUM],
            )
            rel_recv[w] = rel_send[w]

        head_term = dot(grad_bf, rel_ref[...], ((1,), (1,))).astype(BF16)
        grads = tail_grad[...] + dot(head_t[...], head_term, ((1,), (0,)))
        acc = to_column(acc_out[...]) + jnp.mean(grads * grads, axis=1, keepdims=True)
        acc_out[...] = to_row(acc)
        emb_out[...] = emb_out[...] - grads * (LEARN_RATE / (jnp.sqrt(acc) + EPSILON))

        wait(q_send.at[s, others], send_sem.at[s, QUERY_OUT])
        wait(q_send.at[s, others], send_sem.at[s, QUERY_IN])
        wait(q_send.at[s, others], send_sem.at[s, GRAD_OUT])
        wait(q_send.at[s, others], send_sem.at[s, GRAD_IN])
        wait(loss_all.at[s, others], send_sem.at[s, LOSS])
        wait(negs.at[s, peers], nsend_sem.at[s, NEG])
        wait(negs.at[s, peers], nsend_sem.at[s, NEG_GRAD])
        return carry

    lax.fori_loop(0, steps, step, 0)

    wait(rel_recv.at[others], xrecv_sem.at[REL_SUM])
    mine = rel_recv[0].astype(F32)
    for j in range(1, wide):
        mine = mine + rel_recv[j].astype(F32)
    rel_group_send[...] = mine
    narrow_start(
        lambda j: rel_group_send, lambda m: rel_group.at[m],
        xsend_sem.at[REL_GROUP], xrecv_sem.at[REL_GROUP],
    )
    rel_group[n] = mine
    wait(rel_group.at[peers], xrecv_sem.at[REL_GROUP])
    summed = rel_group[0]
    for k in range(1, narrow):
        summed = summed + rel_group[k]
    rel_all_send[...] = summed.astype(BF16)
    wide_start(
        lambda j: rel_all_send, lambda m: rel_all.at[m],
        xsend_sem.at[REL_ALL], xrecv_sem.at[REL_ALL],
    )
    rel_all[w] = rel_all_send[...]
    wait(rel_all.at[others], xrecv_sem.at[REL_ALL])
    rel_out[...] = rel_all[...].astype(F32).reshape(rel_out.shape)

    wait(tail_all.at[others], xsend_sem.at[TAIL_IDS])
    wait(neg_all.at[others], xsend_sem.at[NEG_IDS])
    wait(rel_recv.at[others], xsend_sem.at[REL_SUM])
    wait(rel_group.at[peers], xsend_sem.at[REL_GROUP])
    wait(rel_all.at[others], xsend_sem.at[REL_ALL])


def invert(order):
    positions = jnp.arange(order.shape[1], dtype=jnp.int32)
    return jnp.sum(
        jnp.where(order[:, :, None] == positions, positions[:, None], 0), axis=1, dtype=jnp.int32
    )


def on_device(
    wide, narrow,
    embeddings, accum, relation, head_index, tail_index, negative_index, partner, edge_count
):
    steps, edges = head_index.shape
    block, width = embeddings.shape
    negatives = negative_index.shape[1]
    piece = edges // wide
    depth = width // wide
    chunk = min(edges, 256)
    vmem = pl.BlockSpec(memory_space=pltpu.VMEM)
    smem = pl.BlockSpec(memory_space=pltpu.SMEM)
    pieces = pltpu.VMEM((steps, wide, piece, width), BF16)
    group = pltpu.VMEM((steps, narrow, negatives, width), BF16)
    sems = pltpu.SemaphoreType.DMA
    new_emb, new_acc, rel_grad, losses = pl.pallas_call(
        functools.partial(kernel, wide, narrow, chunk),
        out_shape=(
            jax.ShapeDtypeStruct(embeddings.shape, F32),
            jax.ShapeDtypeStruct((1, block), F32),
            jax.ShapeDtypeStruct(relation.shape, F32),
            jax.ShapeDtypeStruct((steps, edges), F32),
        ),
        in_specs=[vmem] * 6 + [smem] * 3,
        out_specs=(vmem,) * 4,
        scratch_shapes=[
            pltpu.VMEM((wide, steps, edges), jnp.int32),
            pltpu.VMEM((wide, steps, negatives), jnp.int32),
            pltpu.VMEM((block, width), BF16),
            pltpu.VMEM((block, edges), BF16),
            pltpu.VMEM((block, edges), BF16),
            pltpu.VMEM((block, negatives), BF16),
            pltpu.VMEM((edges, width), BF16),
            pltpu.VMEM((edges, width), BF16),
            *([pieces] * 8),
            pltpu.VMEM((steps, 1, edges), F32),
            pltpu.VMEM((steps, wide, 1, edges), F32),
            group, group, group,
            pltpu.VMEM((edges, narrow * negatives), BF16),
            pltpu.VMEM((edges, width), BF16),
            pltpu.VMEM((block, width), F32),
            pltpu.VMEM(relation.shape, F32),
            pltpu.VMEM((wide, depth, width), BF16),
            pltpu.VMEM((wide, depth, width), BF16),
            pltpu.VMEM((depth, width), F32),
            pltpu.VMEM((narrow, depth, width), F32),
            pltpu.VMEM((depth, width), BF16),
            pltpu.VMEM((wide, depth, width), BF16),
            sems((steps, 5)), sems((steps, 5)), sems((steps, 2)), sems((steps, 2)),
            sems((5,)), sems((5,)),
        ],
        compiler_params=pltpu.CompilerParams(
            collective_id=0, has_side_effects=True, vmem_limit_bytes=56 * 1024 * 1024
        ),
    )(
        embeddings, accum.reshape(1, block), relation, head_index, tail_index, negative_index,
        partner, invert(partner), edge_count,
    )
    return new_emb, new_acc.reshape(block), rel_grad, losses


def solution(mesh):
    both = ("wide", "narrow")
    in_specs = (
        P(both, None), P(both), P(), P(None, both), P(None, both), P(None, both), P(), P(None, both)
    )
    out_specs = (P(both, None), P(both), P(), P(None, both))
    return jax.shard_map(
        functools.partial(on_device, mesh.shape["wide"], mesh.shape["narrow"]),
        mesh=mesh, in_specs=in_specs, out_specs=out_specs, check_vma=False,
    )
```

```python
import functools

import jax
import jax.numpy as jnp
from jax import lax
from jax.experimental import pallas as pl
from jax.experimental.pallas import tpu as pltpu
from jax.sharding import PartitionSpec as P

LEARN_RATE = 0.1
EPSILON = 1e-06
MESH = pl.DeviceIdType.MESH
F32 = jnp.float32
BF16 = jnp.bfloat16

QUERY_OUT, QUERY_IN, GRAD_OUT, GRAD_IN, LOSS = range(5)
NEG, NEG_GRAD = range(2)
TAIL_IDS, NEG_IDS, REL_SUM, REL_GROUP, REL_ALL = range(5)
HALVES = 2


def dot(a, b, contract):
    return lax.dot_general(a, b, (contract, ((), ())), preferred_element_type=F32)


def one_hot_t(row, rows):
    number = lax.broadcasted_iota(jnp.int32, (rows, row.shape[1]), 0)
    return jnp.where(number == row, 1.0, 0.0).astype(BF16)


def to_row(column):
    return jnp.transpose(jnp.broadcast_to(column, (column.shape[0], 128)))[:1, :]


def to_column(row):
    return jnp.transpose(jnp.broadcast_to(row, (128, row.shape[1])))[:, :1]


def kernel(
    wide, narrow, chunk,
    emb_ref, acc_ref, rel_ref, head_ref, tail_ref, neg_ref, partner_ref, inverse_ref, count_ref,
    emb_out, acc_out, rel_out, loss_out,
    tail_all, neg_all, table, head_t, tail_t, neg_t, head_rows, tail_rows,
    q_send, q_mid, q_mid_send, q_recv, g_send, g_mid, g_mid_send, g_recv,
    loss_send, loss_all, negs, ng_send, ng_recv, weights, tail_pos, tail_grad,
    rel_acc, rel_send, rel_recv, rel_group_send, rel_group, rel_all_send, rel_all,
    send_sem, recv_sem, nsend_sem, nrecv_sem, xsend_sem, xrecv_sem,
):
    w = lax.axis_index("wide")
    n = lax.axis_index("narrow")
    steps, edges = head_ref.shape
    block, width = emb_ref.shape
    negatives = neg_ref.shape[1]
    parts = edges // chunk
    half = width // HALVES

    barrier = pltpu.get_barrier_semaphore()

    def greet_wide(i, carry):
        pl.semaphore_signal(
            barrier, inc=1, device_id=(lax.rem(w + i, wide), n), device_id_type=MESH
        )
        return carry

    def greet_narrow(i, carry):
        pl.semaphore_signal(
            barrier, inc=1, device_id=(w, lax.rem(n + i, narrow)), device_id_type=MESH
        )
        return carry

    lax.fori_loop(1, wide, greet_wide, 0)
    lax.fori_loop(1, narrow, greet_narrow, 0)
    pl.semaphore_wait(barrier, wide + narrow - 2)

    def wide_start(source, target, ssem, rsem):
        def go(i, carry):
            j = lax.rem(w + i, wide)
            pltpu.make_async_remote_copy(
                src_ref=source(j), dst_ref=target(w), send_sem=ssem, recv_sem=rsem,
                device_id=(j, n), device_id_type=MESH,
            ).start()
            return carry

        lax.fori_loop(1, wide, go, 0)

    def narrow_start(source, target, ssem, rsem):
        def go(i, carry):
            j = lax.rem(n + i, narrow)
            pltpu.make_async_remote_copy(
                src_ref=source(j), dst_ref=target(n), send_sem=ssem, recv_sem=rsem,
                device_id=(w, j), device_id_type=MESH,
            ).start()
            return carry

        lax.fori_loop(1, narrow, go, 0)

    def wait(slots, sem):
        pltpu.make_async_copy(slots, slots, sem).wait()

    def exchange(source, target, s, c, phase):
        wide_start(
            lambda j: source.at[s, c, j], lambda m: target.at[s, m],
            send_sem.at[s, c, phase], recv_sem.at[s, c, phase],
        )
        target[s, w] = source[s, c, w]

    wide_start(
        lambda j: tail_ref, lambda m: tail_all.at[m], xsend_sem.at[0, TAIL_IDS], xrecv_sem.at[0, TAIL_IDS]
    )
    wide_start(
        lambda j: neg_ref, lambda m: neg_all.at[m], xsend_sem.at[0, NEG_IDS], xrecv_sem.at[0, NEG_IDS]
    )
    tail_all[w] = tail_ref[...]
    neg_all[w] = neg_ref[...]
    emb_out[...] = emb_ref[...]
    acc_out[...] = acc_ref[...]
    rel_acc[...] = jnp.zeros_like(rel_acc)
    others = pl.ds(0, wide - 1)
    peers = pl.ds(0, narrow - 1)

    def step(s, carry):
        row = pl.ds(s, 1)
        count = count_ref[s, 0]
        table[...] = emb_out[...].astype(BF16)
        head_t[...] = one_hot_t(head_ref[row, :], block)
        for c in range(parts):
            part = slice(c * chunk, (c + 1) * chunk)
            rows = dot(head_t[:, part], table[...], ((0,), (0,))).astype(BF16)
            head_rows[part, :] = rows
            query = dot(rows, rel_ref[...], ((1,), (0,)))
            live = lax.broadcasted_iota(jnp.int32, (chunk, width), 0) + c * chunk < count
            q_send[s, c] = jnp.where(live, query, 0.0).astype(BF16).reshape(q_send.shape[2:])
            exchange(q_send, q_mid[c], s, c, QUERY_OUT)
        @pl.when(s == 0)
        def _():
            wait(tail_all.at[others], xrecv_sem.at[0, TAIL_IDS])
            wait(neg_all.at[others], xrecv_sem.at[0, NEG_IDS])

        user = inverse_ref[s, w]
        neg_t[...] = one_hot_t(neg_all[user, row, :], block)
        negs[s, n] = dot(neg_t[...], table[...], ((0,), (0,))).astype(BF16)
        narrow_start(
            lambda j: negs.at[s, n], lambda m: negs.at[s, m],
            nsend_sem.at[s, NEG], nrecv_sem.at[s, NEG],
        )
        tail_t[...] = one_hot_t(tail_all[user, row, :], block)
        tail_rows[...] = dot(tail_t[...], table[...], ((0,), (0,))).astype(BF16)

        for c in range(parts):
            wait(q_mid[c].at[s, others], recv_sem.at[s, c, QUERY_OUT])

            def relay_query(j, carry, c=c):
                q_mid_send[s, c, j] = q_mid[c][s, inverse_ref[s, j]]
                return carry

            lax.fori_loop(0, wide, relay_query, 0)
            exchange(q_mid_send, q_recv[c], s, c, QUERY_IN)
        wait(negs.at[s, peers], nrecv_sem.at[s, NEG])

        shared = negs[s].reshape(narrow * negatives, width)
        for c in range(parts):
            part = slice(c * chunk, (c + 1) * chunk)
            wait(q_recv[c].at[s, others], recv_sem.at[s, c, QUERY_IN])
            q = q_recv[c][s].reshape(chunk, width)
            q32 = q.astype(F32)
            t32 = tail_rows[part, :].astype(F32)
            positive = jnp.sum(q32 * t32, axis=1, keepdims=True)
            exp_neg = jnp.exp(dot(q, shared, ((1,), (1,))))
            exp_pos = jnp.exp(positive)
            total = exp_pos + jnp.sum(exp_neg, axis=1, keepdims=True)
            pos_weight = exp_pos / total - 1.0
            wts = (exp_neg * (1.0 / total)).astype(BF16)
            weights[part, :] = wts
            grad = pos_weight * t32 + dot(wts, shared, ((1,), (0,)))
            g_send[s, c] = grad.astype(BF16).reshape(g_send.shape[2:])
            exchange(g_send, g_mid[c], s, c, GRAD_OUT)
            tail_pos[part, :] = (pos_weight * q32).astype(BF16)
            loss_send[s, :, part] = to_row(jnp.log(total) - positive)
        for k in range(narrow):
            cols = slice(k * negatives, (k + 1) * negatives)
            term = jnp.zeros((negatives, width), F32)
            for c in range(parts):
                part = slice(c * chunk, (c + 1) * chunk)
                queries = q_recv[c][s].reshape(chunk, width)
                term = term + dot(weights[part, cols], queries, ((0,), (0,)))
            ng_send[s, k] = term.astype(BF16)
        narrow_start(
            lambda j: ng_send.at[s, j], lambda m: ng_recv.at[s, m],
            nsend_sem.at[s, NEG_GRAD], nrecv_sem.at[s, NEG_GRAD],
        )
        ng_recv[s, n] = ng_send[s, n]
        wide_start(
            lambda j: loss_send.at[s], lambda m: loss_all.at[s, m],
            send_sem.at[s, 0, LOSS], recv_sem.at[s, 0, LOSS],
        )
        loss_all[s, w] = loss_send[s]
        tail_grad[...] = dot(tail_t[...], tail_pos[...], ((1,), (0,)))

        for c in range(parts):
            wait(g_mid[c].at[s, others], recv_sem.at[s, c, GRAD_OUT])

            def relay_grad(j, carry, c=c):
                g_mid_send[s, c, j] = g_mid[c][s, partner_ref[s, j]]
                return carry

            lax.fori_loop(0, wide, relay_grad, 0)
            exchange(g_mid_send, g_recv[c], s, c, GRAD_IN)

        wait(ng_recv.at[s, peers], nrecv_sem.at[s, NEG_GRAD])
        for k in range(narrow):
            tail_grad[...] += dot(neg_t[...], ng_recv[s, k], ((1,), (0,)))
        wait(loss_all.at[s, others], recv_sem.at[s, 0, LOSS])
        losses = loss_all[s, partner_ref[s, w]]
        live_row = lax.broadcasted_iota(jnp.int32, (1, edges), 1) < count
        loss_out[row, :] = jnp.where(live_row, losses, 0.0)

        for c in range(parts):
            part = slice(c * chunk, (c + 1) * chunk)
            wait(g_recv[c].at[s, others], recv_sem.at[s, c, GRAD_IN])
            back = g_recv[c][s].reshape(chunk, width).astype(F32)
            live = lax.broadcasted_iota(jnp.int32, (chunk, width), 0) + c * chunk < count
            grad_bf = jnp.where(live, back, 0.0).astype(BF16)
            rel_acc[...] += dot(head_rows[part, :], grad_bf, ((0,), (0,)))
            tail_pos[part, :] = dot(grad_bf, rel_ref[...], ((1,), (1,))).astype(BF16)

        @pl.when(s == steps - 1)
        def _():
            for h in range(HALVES):
                cols = slice(h * half, (h + 1) * half)
                rel_send[h] = rel_acc[:, cols].astype(BF16).reshape(rel_send.shape[1:])
                wide_start(
                    lambda j: rel_send.at[h, j], lambda m: rel_recv.at[h, m],
                    xsend_sem.at[h, REL_SUM], xrecv_sem.at[h, REL_SUM],
                )
                rel_recv[h, w] = rel_send[h, w]

        grads = tail_grad[...] + dot(head_t[...], tail_pos[...], ((1,), (0,)))
        acc = to_column(acc_out[...]) + jnp.mean(grads * grads, axis=1, keepdims=True)
        acc_out[...] = to_row(acc)
        emb_out[...] = emb_out[...] - grads * (LEARN_RATE / (jnp.sqrt(acc) + EPSILON))

        for c in range(parts):
            for phase in (QUERY_OUT, QUERY_IN, GRAD_OUT, GRAD_IN):
                wait(q_send.at[s, c, others], send_sem.at[s, c, phase])
        wait(loss_all.at[s, others], send_sem.at[s, 0, LOSS])
        wait(negs.at[s, peers], nsend_sem.at[s, NEG])
        wait(negs.at[s, peers], nsend_sem.at[s, NEG_GRAD])
        return carry

    lax.fori_loop(0, steps, step, 0)

    for h in range(HALVES):
        wait(rel_recv.at[h, others], xrecv_sem.at[h, REL_SUM])
        mine = rel_recv[h, 0].astype(F32)
        for j in range(1, wide):
            mine = mine + rel_recv[h, j].astype(F32)
        rel_group_send[h] = mine
        narrow_start(
            lambda j: rel_group_send.at[h], lambda m: rel_group.at[h, m],
            xsend_sem.at[h, REL_GROUP], xrecv_sem.at[h, REL_GROUP],
        )
        rel_group[h, n] = mine
    for h in range(HALVES):
        wait(rel_group.at[h, peers], xrecv_sem.at[h, REL_GROUP])
        summed = rel_group[h, 0]
        for k in range(1, narrow):
            summed = summed + rel_group[h, k]
        rel_all_send[h] = summed.astype(BF16)
        wide_start(
            lambda j: rel_all_send.at[h], lambda m: rel_all.at[h, m],
            xsend_sem.at[h, REL_ALL], xrecv_sem.at[h, REL_ALL],
        )
        rel_all[h, w] = rel_all_send[h]
    for h in range(HALVES):
        wait(rel_all.at[h, others], xrecv_sem.at[h, REL_ALL])
        rel_out[:, h * half:(h + 1) * half] = rel_all[h].astype(F32).reshape(width, half)

    wait(tail_all.at[others], xsend_sem.at[0, TAIL_IDS])
    wait(neg_all.at[others], xsend_sem.at[0, NEG_IDS])
    for h in range(HALVES):
        wait(rel_recv.at[h, others], xsend_sem.at[h, REL_SUM])
        wait(rel_group.at[h, peers], xsend_sem.at[h, REL_GROUP])
        wait(rel_all.at[h, others], xsend_sem.at[h, REL_ALL])


def invert(order):
    positions = jnp.arange(order.shape[1], dtype=jnp.int32)
    return jnp.sum(
        jnp.where(order[:, :, None] == positions, positions[:, None], 0), axis=1, dtype=jnp.int32
    )


def on_device(
    wide, narrow,
    embeddings, accum, relation, head_index, tail_index, negative_index, partner, edge_count
):
    steps, edges = head_index.shape
    block, width = embeddings.shape
    negatives = negative_index.shape[1]
    depth = width // wide
    parts = max(1, min(2, edges // (16 * wide)))
    chunk = edges // parts
    piece = chunk // wide
    half = width // HALVES
    vmem = pl.BlockSpec(memory_space=pltpu.VMEM)
    smem = pl.BlockSpec(memory_space=pltpu.SMEM)
    pieces = pltpu.VMEM((steps, parts, wide, piece, width), BF16)
    landing = pltpu.VMEM((steps, wide, piece, width), BF16)
    group = pltpu.VMEM((steps, narrow, negatives, width), BF16)
    sems = pltpu.SemaphoreType.DMA
    new_emb, new_acc, rel_grad, losses = pl.pallas_call(
        functools.partial(kernel, wide, narrow, chunk),
        out_shape=(
            jax.ShapeDtypeStruct(embeddings.shape, F32),
            jax.ShapeDtypeStruct((1, block), F32),
            jax.ShapeDtypeStruct(relation.shape, F32),
            jax.ShapeDtypeStruct((steps, edges), F32),
        ),
        in_specs=[vmem] * 6 + [smem] * 3,
        out_specs=(vmem,) * 4,
        scratch_shapes=[
            pltpu.VMEM((wide, steps, edges), jnp.int32),
            pltpu.VMEM((wide, steps, negatives), jnp.int32),
            pltpu.VMEM((block, width), BF16),
            pltpu.VMEM((block, edges), BF16),
            pltpu.VMEM((block, edges), BF16),
            pltpu.VMEM((block, negatives), BF16),
            pltpu.VMEM((edges, width), BF16),
            pltpu.VMEM((edges, width), BF16),
            pieces, [landing] * parts, pieces, [landing] * parts,
            pieces, [landing] * parts, pieces, [landing] * parts,
            pltpu.VMEM((steps, 1, edges), F32),
            pltpu.VMEM((steps, wide, 1, edges), F32),
            group, group, group,
            pltpu.VMEM((edges, narrow * negatives), BF16),
            pltpu.VMEM((edges, width), BF16),
            pltpu.VMEM((block, width), F32),
            pltpu.VMEM(relation.shape, F32),
            pltpu.VMEM((HALVES, wide, depth, half), BF16),
            pltpu.VMEM((HALVES, wide, depth, half), BF16),
            pltpu.VMEM((HALVES, depth, half), F32),
            pltpu.VMEM((HALVES, narrow, depth, half), F32),
            pltpu.VMEM((HALVES, depth, half), BF16),
            pltpu.VMEM((HALVES, wide, depth, half), BF16),
            sems((steps, parts, 5)), sems((steps, parts, 5)), sems((steps, 2)), sems((steps, 2)),
            sems((HALVES, 5)), sems((HALVES, 5)),
        ],
        compiler_params=pltpu.CompilerParams(
            collective_id=0, has_side_effects=True, vmem_limit_bytes=56 * 1024 * 1024
        ),
    )(
        embeddings, accum.reshape(1, block), relation, head_index, tail_index, negative_index,
        partner, invert(partner), edge_count,
    )
    return new_emb, new_acc.reshape(block), rel_grad, losses


def solution(mesh):
    both = ("wide", "narrow")
    in_specs = (
        P(both, None), P(both), P(), P(None, both), P(None, both), P(None, both), P(), P(None, both)
    )
    out_specs = (P(both, None), P(both), P(), P(None, both))
    return jax.shard_map(
        functools.partial(on_device, mesh.shape["wide"], mesh.shape["narrow"]),
        mesh=mesh, in_specs=in_specs, out_specs=out_specs, check_vma=False,
    )
```

```python
import functools

import jax
import jax.numpy as jnp
from jax import lax
from jax.experimental import pallas as pl
from jax.experimental.pallas import tpu as pltpu
from jax.sharding import PartitionSpec as P

LEARN_RATE = 0.1
EPSILON = 1e-06
MESH = pl.DeviceIdType.MESH
F32 = jnp.float32
BF16 = jnp.bfloat16

QUERY_OUT, QUERY_IN, GRAD_OUT, GRAD_IN, LOSS = range(5)
NEG, NEG_GRAD = range(2)
TAIL_IDS, NEG_IDS, REL_SUM, REL_GROUP, REL_ALL = range(5)
HALVES = 2


def dot(a, b, contract):
    return lax.dot_general(a, b, (contract, ((), ())), preferred_element_type=F32)


def one_hot_t(row, rows):
    number = lax.broadcasted_iota(jnp.int32, (rows, row.shape[1]), 0)
    return jnp.where(number == row, 1.0, 0.0).astype(BF16)


def to_row(column):
    return jnp.transpose(jnp.broadcast_to(column, (column.shape[0], 128)))[:1, :]


def to_column(row):
    return jnp.transpose(jnp.broadcast_to(row, (128, row.shape[1])))[:, :1]


def kernel(
    wide, narrow, chunk,
    emb_ref, acc_ref, rel_ref, head_ref, tail_ref, neg_ref, partner_ref, inverse_ref, count_ref,
    emb_out, acc_out, rel_out, loss_out,
    tail_all, neg_all, table, head_t, tail_t, neg_t, head_rows, tail_rows,
    q_send, q_mid, q_mid_send, q_recv, g_send, g_mid, g_mid_send, g_recv,
    loss_send, loss_all, negs, ng_send, ng_recv, weights, tail_pos, tail_grad,
    rel_acc, rel_send, rel_recv, rel_group_send, rel_group, rel_all_send, rel_all,
    send_sem, recv_sem, nsend_sem, nrecv_sem, xsend_sem, xrecv_sem,
):
    w = lax.axis_index("wide")
    n = lax.axis_index("narrow")
    steps, edges = head_ref.shape
    block, width = emb_ref.shape
    negatives = neg_ref.shape[1]
    parts = edges // chunk
    half = width // HALVES

    barrier = pltpu.get_barrier_semaphore()

    def greet_wide(i, carry):
        pl.semaphore_signal(
            barrier, inc=1, device_id=(lax.rem(w + i, wide), n), device_id_type=MESH
        )
        return carry

    def greet_narrow(i, carry):
        pl.semaphore_signal(
            barrier, inc=1, device_id=(w, lax.rem(n + i, narrow)), device_id_type=MESH
        )
        return carry

    lax.fori_loop(1, wide, greet_wide, 0)
    lax.fori_loop(1, narrow, greet_narrow, 0)
    pl.semaphore_wait(barrier, wide + narrow - 2)

    def wide_start(source, target, ssem, rsem):
        def go(i, carry):
            far = 1 + lax.rem(i - 1 + (wide - 1) // 2, wide - 1)
            j = lax.rem(w + far, wide)
            pltpu.make_async_remote_copy(
                src_ref=source(j), dst_ref=target(w), send_sem=ssem, recv_sem=rsem,
                device_id=(j, n), device_id_type=MESH,
            ).start()
            return carry

        lax.fori_loop(1, wide, go, 0)

    def narrow_start(source, target, ssem, rsem):
        def go(i, carry):
            j = lax.rem(n + i, narrow)
            pltpu.make_async_remote_copy(
                src_ref=source(j), dst_ref=target(n), send_sem=ssem, recv_sem=rsem,
                device_id=(w, j), device_id_type=MESH,
            ).start()
            return carry

        lax.fori_loop(1, narrow, go, 0)

    def wait(slots, sem):
        pltpu.make_async_copy(slots, slots, sem).wait()

    def exchange(source, target, s, c, phase):
        wide_start(
            lambda j: source.at[s, c, j], lambda m: target.at[s, m],
            send_sem.at[s, c, phase], recv_sem.at[s, c, phase],
        )
        target[s, w] = source[s, c, w]

    wide_start(
        lambda j: tail_ref, lambda m: tail_all.at[m], xsend_sem.at[0, TAIL_IDS], xrecv_sem.at[0, TAIL_IDS]
    )
    wide_start(
        lambda j: neg_ref, lambda m: neg_all.at[m], xsend_sem.at[0, NEG_IDS], xrecv_sem.at[0, NEG_IDS]
    )
    tail_all[w] = tail_ref[...]
    neg_all[w] = neg_ref[...]
    emb_out[...] = emb_ref[...]
    acc_out[...] = acc_ref[...]
    rel_acc[...] = jnp.zeros_like(rel_acc)
    others = pl.ds(0, wide - 1)
    peers = pl.ds(0, narrow - 1)

    def step(s, carry):
        row = pl.ds(s, 1)
        count = count_ref[s, 0]
        table[...] = emb_out[...].astype(BF16)
        head_t[...] = one_hot_t(head_ref[row, :], block)
        for c in range(parts):
            part = slice(c * chunk, (c + 1) * chunk)
            rows = dot(head_t[:, part], table[...], ((0,), (0,))).astype(BF16)
            head_rows[part, :] = rows
            query = dot(rows, rel_ref[...], ((1,), (0,)))
            live = lax.broadcasted_iota(jnp.int32, (chunk, width), 0) + c * chunk < count
            q_send[s, c] = jnp.where(live, query, 0.0).astype(BF16).reshape(q_send.shape[2:])
            exchange(q_send, q_mid[c], s, c, QUERY_OUT)
        @pl.when(s == 0)
        def _():
            wait(tail_all.at[others], xrecv_sem.at[0, TAIL_IDS])
            wait(neg_all.at[others], xrecv_sem.at[0, NEG_IDS])

        user = inverse_ref[s, w]
        neg_t[...] = one_hot_t(neg_all[user, row, :], block)
        negs[s, n] = dot(neg_t[...], table[...], ((0,), (0,))).astype(BF16)
        narrow_start(
            lambda j: negs.at[s, n], lambda m: negs.at[s, m],
            nsend_sem.at[s, NEG], nrecv_sem.at[s, NEG],
        )
        tail_t[...] = one_hot_t(tail_all[user, row, :], block)
        tail_rows[...] = dot(tail_t[...], table[...], ((0,), (0,))).astype(BF16)

        for c in range(parts):
            wait(q_mid[c].at[s, others], recv_sem.at[s, c, QUERY_OUT])

            def relay_query(j, carry, c=c):
                q_mid_send[s, c, j] = q_mid[c][s, inverse_ref[s, j]]
                return carry

            lax.fori_loop(0, wide, relay_query, 0)
            exchange(q_mid_send, q_recv[c], s, c, QUERY_IN)
        wait(negs.at[s, peers], nrecv_sem.at[s, NEG])

        shared = negs[s].reshape(narrow * negatives, width)
        for c in range(parts):
            part = slice(c * chunk, (c + 1) * chunk)
            wait(q_recv[c].at[s, others], recv_sem.at[s, c, QUERY_IN])
            q = q_recv[c][s].reshape(chunk, width)
            q32 = q.astype(F32)
            t32 = tail_rows[part, :].astype(F32)
            positive = jnp.sum(q32 * t32, axis=1, keepdims=True)
            exp_neg = jnp.exp(dot(q, shared, ((1,), (1,))))
            exp_pos = jnp.exp(positive)
            total = exp_pos + jnp.sum(exp_neg, axis=1, keepdims=True)
            pos_weight = exp_pos / total - 1.0
            wts = (exp_neg * (1.0 / total)).astype(BF16)
            weights[part, :] = wts
            grad = pos_weight * t32 + dot(wts, shared, ((1,), (0,)))
            g_send[s, c] = grad.astype(BF16).reshape(g_send.shape[2:])
            exchange(g_send, g_mid[c], s, c, GRAD_OUT)
            tail_pos[part, :] = (pos_weight * q32).astype(BF16)
            loss_send[s, :, part] = to_row(jnp.log(total) - positive)
        for k in range(narrow):
            cols = slice(k * negatives, (k + 1) * negatives)
            term = jnp.zeros((negatives, width), F32)
            for c in range(parts):
                part = slice(c * chunk, (c + 1) * chunk)
                queries = q_recv[c][s].reshape(chunk, width)
                term = term + dot(weights[part, cols], queries, ((0,), (0,)))
            ng_send[s, k] = term.astype(BF16)
        narrow_start(
            lambda j: ng_send.at[s, j], lambda m: ng_recv.at[s, m],
            nsend_sem.at[s, NEG_GRAD], nrecv_sem.at[s, NEG_GRAD],
        )
        ng_recv[s, n] = ng_send[s, n]
        wide_start(
            lambda j: loss_send.at[s], lambda m: loss_all.at[s, m],
            send_sem.at[s, 0, LOSS], recv_sem.at[s, 0, LOSS],
        )
        loss_all[s, w] = loss_send[s]
        tail_grad[...] = dot(tail_t[...], tail_pos[...], ((1,), (0,)))

        for c in range(parts):
            wait(g_mid[c].at[s, others], recv_sem.at[s, c, GRAD_OUT])

            def relay_grad(j, carry, c=c):
                g_mid_send[s, c, j] = g_mid[c][s, partner_ref[s, j]]
                return carry

            lax.fori_loop(0, wide, relay_grad, 0)
            exchange(g_mid_send, g_recv[c], s, c, GRAD_IN)

        wait(ng_recv.at[s, peers], nrecv_sem.at[s, NEG_GRAD])
        for k in range(narrow):
            tail_grad[...] += dot(neg_t[...], ng_recv[s, k], ((1,), (0,)))
        wait(loss_all.at[s, others], recv_sem.at[s, 0, LOSS])
        losses = loss_all[s, partner_ref[s, w]]
        live_row = lax.broadcasted_iota(jnp.int32, (1, edges), 1) < count
        loss_out[row, :] = jnp.where(live_row, losses, 0.0)

        for c in range(parts):
            part = slice(c * chunk, (c + 1) * chunk)
            wait(g_recv[c].at[s, others], recv_sem.at[s, c, GRAD_IN])
            back = g_recv[c][s].reshape(chunk, width).astype(F32)
            live = lax.broadcasted_iota(jnp.int32, (chunk, width), 0) + c * chunk < count
            grad_bf = jnp.where(live, back, 0.0).astype(BF16)
            rel_acc[...] += dot(head_rows[part, :], grad_bf, ((0,), (0,)))
            tail_pos[part, :] = dot(grad_bf, rel_ref[...], ((1,), (1,))).astype(BF16)

        @pl.when(s == steps - 1)
        def _():
            for h in range(HALVES):
                cols = slice(h * half, (h + 1) * half)
                rel_send[h] = rel_acc[:, cols].astype(BF16).reshape(rel_send.shape[1:])
                wide_start(
                    lambda j: rel_send.at[h, j], lambda m: rel_recv.at[h, m],
                    xsend_sem.at[h, REL_SUM], xrecv_sem.at[h, REL_SUM],
                )
                rel_recv[h, w] = rel_send[h, w]

        grads = tail_grad[...] + dot(head_t[...], tail_pos[...], ((1,), (0,)))
        acc = to_column(acc_out[...]) + jnp.mean(grads * grads, axis=1, keepdims=True)
        acc_out[...] = to_row(acc)
        emb_out[...] = emb_out[...] - grads * (LEARN_RATE / (jnp.sqrt(acc) + EPSILON))

        for c in range(parts):
            for phase in (QUERY_OUT, QUERY_IN, GRAD_OUT, GRAD_IN):
                wait(q_send.at[s, c, others], send_sem.at[s, c, phase])
        wait(loss_all.at[s, others], send_sem.at[s, 0, LOSS])
        wait(negs.at[s, peers], nsend_sem.at[s, NEG])
        wait(negs.at[s, peers], nsend_sem.at[s, NEG_GRAD])
        return carry

    lax.fori_loop(0, steps, step, 0)

    for h in range(HALVES):
        wait(rel_recv.at[h, others], xrecv_sem.at[h, REL_SUM])
        mine = rel_recv[h, 0].astype(F32)
        for j in range(1, wide):
            mine = mine + rel_recv[h, j].astype(F32)
        rel_group_send[h] = mine
        narrow_start(
            lambda j: rel_group_send.at[h], lambda m: rel_group.at[h, m],
            xsend_sem.at[h, REL_GROUP], xrecv_sem.at[h, REL_GROUP],
        )
        rel_group[h, n] = mine
    for h in range(HALVES):
        wait(rel_group.at[h, peers], xrecv_sem.at[h, REL_GROUP])
        summed = rel_group[h, 0]
        for k in range(1, narrow):
            summed = summed + rel_group[h, k]
        rel_all_send[h] = summed.astype(BF16)
        wide_start(
            lambda j: rel_all_send.at[h], lambda m: rel_all.at[h, m],
            xsend_sem.at[h, REL_ALL], xrecv_sem.at[h, REL_ALL],
        )
        rel_all[h, w] = rel_all_send[h]
    for h in range(HALVES):
        wait(rel_all.at[h, others], xrecv_sem.at[h, REL_ALL])
        rel_out[:, h * half:(h + 1) * half] = rel_all[h].astype(F32).reshape(width, half)

    wait(tail_all.at[others], xsend_sem.at[0, TAIL_IDS])
    wait(neg_all.at[others], xsend_sem.at[0, NEG_IDS])
    for h in range(HALVES):
        wait(rel_recv.at[h, others], xsend_sem.at[h, REL_SUM])
        wait(rel_group.at[h, peers], xsend_sem.at[h, REL_GROUP])
        wait(rel_all.at[h, others], xsend_sem.at[h, REL_ALL])


def invert(order):
    positions = jnp.arange(order.shape[1], dtype=jnp.int32)
    return jnp.sum(
        jnp.where(order[:, :, None] == positions, positions[:, None], 0), axis=1, dtype=jnp.int32
    )


def on_device(
    wide, narrow,
    embeddings, accum, relation, head_index, tail_index, negative_index, partner, edge_count
):
    steps, edges = head_index.shape
    block, width = embeddings.shape
    negatives = negative_index.shape[1]
    depth = width // wide
    parts = max(1, min(2, edges // (16 * wide)))
    chunk = edges // parts
    piece = chunk // wide
    half = width // HALVES
    vmem = pl.BlockSpec(memory_space=pltpu.VMEM)
    smem = pl.BlockSpec(memory_space=pltpu.SMEM)
    pieces = pltpu.VMEM((steps, parts, wide, piece, width), BF16)
    landing = pltpu.VMEM((steps, wide, piece, width), BF16)
    group = pltpu.VMEM((steps, narrow, negatives, width), BF16)
    sems = pltpu.SemaphoreType.DMA
    new_emb, new_acc, rel_grad, losses = pl.pallas_call(
        functools.partial(kernel, wide, narrow, chunk),
        out_shape=(
            jax.ShapeDtypeStruct(embeddings.shape, F32),
            jax.ShapeDtypeStruct((1, block), F32),
            jax.ShapeDtypeStruct(relation.shape, F32),
            jax.ShapeDtypeStruct((steps, edges), F32),
        ),
        in_specs=[vmem] * 6 + [smem] * 3,
        out_specs=(vmem,) * 4,
        scratch_shapes=[
            pltpu.VMEM((wide, steps, edges), jnp.int32),
            pltpu.VMEM((wide, steps, negatives), jnp.int32),
            pltpu.VMEM((block, width), BF16),
            pltpu.VMEM((block, edges), BF16),
            pltpu.VMEM((block, edges), BF16),
            pltpu.VMEM((block, negatives), BF16),
            pltpu.VMEM((edges, width), BF16),
            pltpu.VMEM((edges, width), BF16),
            pieces, [landing] * parts, pieces, [landing] * parts,
            pieces, [landing] * parts, pieces, [landing] * parts,
            pltpu.VMEM((steps, 1, edges), F32),
            pltpu.VMEM((steps, wide, 1, edges), F32),
            group, group, group,
            pltpu.VMEM((edges, narrow * negatives), BF16),
            pltpu.VMEM((edges, width), BF16),
            pltpu.VMEM((block, width), F32),
            pltpu.VMEM(relation.shape, F32),
            pltpu.VMEM((HALVES, wide, depth, half), BF16),
            pltpu.VMEM((HALVES, wide, depth, half), BF16),
            pltpu.VMEM((HALVES, depth, half), F32),
            pltpu.VMEM((HALVES, narrow, depth, half), F32),
            pltpu.VMEM((HALVES, depth, half), BF16),
            pltpu.VMEM((HALVES, wide, depth, half), BF16),
            sems((steps, parts, 5)), sems((steps, parts, 5)), sems((steps, 2)), sems((steps, 2)),
            sems((HALVES, 5)), sems((HALVES, 5)),
        ],
        compiler_params=pltpu.CompilerParams(
            collective_id=0, has_side_effects=True, vmem_limit_bytes=56 * 1024 * 1024
        ),
    )(
        embeddings, accum.reshape(1, block), relation, head_index, tail_index, negative_index,
        partner, invert(partner), edge_count,
    )
    return new_emb, new_acc.reshape(block), rel_grad, losses


def solution(mesh):
    both = ("wide", "narrow")
    in_specs = (
        P(both, None), P(both), P(), P(None, both), P(None, both), P(None, both), P(), P(None, both)
    )
    out_specs = (P(both, None), P(both), P(), P(None, both))
    return jax.shard_map(
        functools.partial(on_device, mesh.shape["wide"], mesh.shape["narrow"]),
        mesh=mesh, in_specs=in_specs, out_specs=out_specs, check_vma=False,
    )
```
